32 devices in a mesh: grp: 2 (over y), aux: 4 (over z), orb: 2 (over x), occ: 2 (over core).
Axes of the slice: x: 2, y: 2, z: 4, core: 2. Of those that a mesh axis runs over, the one named last changes fastest.
Arguments:
- b_tiles: bfloat16 [64, 32, 4, 128, 128], P(('grp', 'aux'), 'orb'), parts along dimension 0, may hold values from -0.25 to 0.25
- nu_block: int32 [64, 32, 4], P(('grp', 'aux'), 'orb'), parts along dimension 0, may hold values from 0 to 31
- tile_mask: int32 [64, 32, 4], P(('grp', 'aux'), 'orb'), parts along dimension 0, may hold values 0 or 1
- assignment: int32 [64], P(('grp', 'aux')), parts along dimension 0, may hold values from 0 to 31, each once
- metric_factor: float32 [64], P('grp'), parts along dimension 0, may hold values from 0.05 to 0.3
- orbitals: bfloat16 [800, 4000], P('grp'), parts along dimension 0, may hold values from -6 to 6
- occupied_index: int32 [64], P(('grp', 'occ')), parts along dimension 0, may hold values from 0 to 399
Outputs:
- exchange: float32 [8192, 4096], P(('grp', 'aux', 'occ'), 'orb'), parts along dimension 0
The draws below stay inside these ranges and needn't reach their ends.
There are 2 independent parts, one for each index of `grp`. The reference program is written for one: setup_inputs(seed, part) draws one part's arguments, and reference() takes and returns one part's arrays. A program takes and returns all parts, laid end to end along the dimension named above; each array names one. Nothing has to cross between parts.
Inputs may be any that keep to these rules, and one draw needn't show every extreme that they name: `nu_block`: each entry names a column block. `assignment`: each number once. `occupied_index`: repeats may occur.
All inputs are finite; a program needn't handle non-finite values. No bound on the sum of `tile_mask` on one device may be relied on, other than what follows from the above.
Results may differ from the reference program's by a relative error of at most 0.0033.
Values may be sent and summed in bfloat16 or wider, within the bound.
A program may use at most 128 MiB of HBM per device.

```python
import math
import jax
import jax.numpy as jnp
from jax import lax

N = 4000
TILE = 128
NOCC = 400
BATCH = 32
SLOTS = 4
NB = 32
NAUX = 32


def touch_ends(result, key, smallest, largest):
    spot = [jax.random.randint(jax.random.fold_in(key, axis), (), 0, length) for axis, length in enumerate(result.shape)]
    widest = result.shape.index(max(result.shape))
    neighbour = spot[:widest] + [(spot[widest] + 1) % result.shape[widest]] + spot[widest + 1:]
    return result.at[tuple(spot)].set(smallest).at[tuple(neighbour)].set(largest)


def levels(own_key, dims, cuts, smallest, largest):
    level = 1.0
    for axis_at, shards_of in cuts:
        steps = jax.random.uniform(jax.random.fold_in(jax.random.fold_in(own_key, 6), axis_at), (shards_of,), jnp.float32, smallest / len(cuts), largest / len(cuts))
        level = level * jnp.repeat(jnp.exp(steps), dims[axis_at] // shards_of).reshape((-1,) + (1,) * (len(dims) - 1 - axis_at))
    return level


def gaussian(stream_key, dims, deviation, reach, cuts=(), held_as=jnp.bfloat16):
    factor_of = levels(stream_key, dims, cuts, -0.22, 0.18) if cuts else 1.0
    array = jax.random.normal(stream_key, dims, jnp.float32) * deviation * factor_of
    return jnp.minimum(jnp.maximum(array, -reach), reach).astype(held_as)


def setup_inputs(seed: int = 0, part: int = 0) -> dict:
    arg_keys = jax.random.split(jax.random.key(seed), 8)
    part_splits = jax.random.split(jax.random.fold_in(arg_keys[7], part), 8)
    return {
        "b_tiles": gaussian(part_splits[0], (NAUX, NB, SLOTS, TILE, TILE), (SLOTS * TILE) ** -0.5, 0.25, ((0, 4), (1, 2))),
        "nu_block": touch_ends(jax.random.randint(part_splits[1], (NAUX, NB, SLOTS), 0, NB), jax.random.fold_in(part_splits[1], 1), 0, NB - 1).astype(jnp.int32),
        "tile_mask": touch_ends((jax.random.randint(part_splits[2], (NAUX, NB, SLOTS), 0, 4) < 3).astype(jnp.int32), jax.random.fold_in(part_splits[2], 1), 0, 1),
        "assignment": jax.random.permutation(part_splits[3], NAUX).astype(jnp.int32),
        "metric_factor": jnp.clip(jnp.exp(jax.random.uniform(part_splits[4], (NAUX,), jnp.float32, math.log(0.05), math.log(0.3))), 0.05, 0.3),
        "orbitals": gaussian(part_splits[5], (NOCC, N), 1.0, 6.0),
        "occupied_index": touch_ends(jax.random.randint(part_splits[6], (BATCH,), 0, NOCC), jax.random.fold_in(part_splits[6], 1), 0, NOCC - 1).astype(jnp.int32),
    }


def reference(b_tiles, nu_block, tile_mask, assignment, metric_factor, orbitals, occupied_index):
    nblocks = (N + TILE - 1) // TILE
    padded = nblocks * TILE
    picked = orbitals[occupied_index].astype(jnp.float32)
    picked = jnp.pad(picked, ((0, 0), (0, padded - N)))
    blocks = picked.reshape(BATCH, nblocks, TILE)
    factors = metric_factor[assignment]
    inside = jnp.arange(padded) < N

    def half_transform(inputs):
        stored, columns, masking, scaled = inputs
        chosen = blocks[:, columns] * masking.astype(jnp.float32)[None, :, :, None]
        product = jnp.einsum("msab,imsb->ima", stored.astype(jnp.float32), chosen, precision=lax.Precision.HIGHEST)
        product = product.reshape(BATCH, padded) * scaled
        return jnp.where(inside[None, :], product, 0.0).astype(jnp.bfloat16)

    slab_list = lax.map(half_transform, (b_tiles, nu_block, tile_mask, factors))
    flattened = slab_list.reshape(-1, padded).astype(jnp.float32)
    return lax.dot_general(flattened, flattened, (((0,), (0,)), ((), ())), precision=lax.Precision.HIGHEST)
```

```python
import functools
import jax
import jax.numpy as jnp
from jax import lax
from jax.experimental import pallas as pl
from jax.experimental.pallas import tpu as pltpu
from jax.sharding import PartitionSpec as P

MESH = pl.DeviceIdType.MESH
HALVES = 2
COL_TILE = 512


def kernel(sizes, picked_ref, column_ref, assign_ref, metric_ref, b_ref, out_ref,
           chosen, stored, slabs, owner, owner_t,
           load_sem, pick_sem, line_send, line_recv, pair_send, pair_recv, orb_send, orb_recv):
    nz, nx, n_basis = sizes
    naux, row_blocks, slots, tile, _ = b_ref.shape
    nblocks, batch_dev, _ = picked_ref.shape
    block_rows, mu_dev = out_ref.shape
    np_dev = naux // 2
    per_half = np_dev // HALVES
    z, x, c = lax.axis_index("aux"), lax.axis_index("orb"), lax.axis_index("occ")
    mate = 1 - c

    def slot_of(origin, p, core):
        return (origin * np_dev + p) * 2 + core

    def root_of(core):
        first = (z * 2 + core) * block_rows
        root = first // mu_dev
        return root, pl.multiple_of(first - root * mu_dev, 128)

    my_root, my_offset = root_of(c)

    def load(p):
        return pltpu.make_async_copy(b_ref.at[c * np_dev + p], stored.at[p], load_sem.at[p])

    for p in range(np_dev):
        load(p).start()

    barrier = pltpu.get_barrier_semaphore()

    def greet(target):
        pl.semaphore_signal(barrier, inc=1, device_id=target, device_id_type=MESH)

    greet({"occ": mate})
    for step in range(1, nx):
        for core in range(2):
            greet({"orb": lax.rem(x + step, nx), "occ": core})

    @pl.when(z > 0)
    def _():
        greet({"aux": z - 1})

    @pl.when(z < nz - 1)
    def _():
        greet({"aux": z + 1})

    chosen[pl.ds(0, nblocks), pl.ds(pl.multiple_of(c * batch_dev, batch_dev), batch_dev), :] = picked_ref[...]
    chosen[nblocks] = jnp.zeros(chosen.shape[1:], chosen.dtype)
    ends = jnp.where(z > 0, 1, 0) + jnp.where(z < nz - 1, 1, 0)
    pl.semaphore_wait(barrier, 1 + 2 * (nx - 1) + ends)

    pick = pltpu.make_async_remote_copy(
        src_ref=picked_ref,
        dst_ref=chosen.at[pl.ds(0, nblocks), pl.ds(pl.multiple_of(c * batch_dev, batch_dev), batch_dev), :],
        send_sem=pick_sem.at[0], recv_sem=pick_sem.at[1],
        device_id={"occ": mate}, device_id_type=MESH)
    pick.start()
    out_ref[...] = jnp.zeros_like(out_ref)

    def line_copy(s, way):
        return pltpu.make_async_remote_copy(
            src_ref=slabs.at[s], dst_ref=slabs.at[s],
            send_sem=line_send.at[way, s], recv_sem=line_recv.at[s],
            device_id={"aux": z + (1 if way == 0 else -1)}, device_id_type=MESH)

    def pair_copy(s):
        return pltpu.make_async_remote_copy(
            src_ref=slabs.at[s], dst_ref=slabs.at[s],
            send_sem=pair_send.at[s], recv_sem=pair_recv.at[s],
            device_id={"occ": mate}, device_id_type=MESH)

    def orb_copy(s, core, step):
        _, offset = root_of(core)
        return pltpu.make_async_remote_copy(
            src_ref=slabs.at[s, :, pl.ds(offset, block_rows)], dst_ref=owner.at[s],
            send_sem=orb_send.at[core, step - 1, s], recv_sem=orb_recv.at[s],
            device_id={"orb": lax.rem(x + step, nx), "occ": core}, device_id_type=MESH)

    def spread(s):
        pair_copy(s).start()
        for core in range(2):
            @pl.when(x == root_of(core)[0])
            def _():
                for step in range(1, nx):
                    orb_copy(s, core, step).start()

    pick.wait()

    def transform(p, carry):
        load(p).wait()
        mine = c * np_dev + p
        factor = metric_ref[assign_ref[mine]]
        s = slot_of(z, p, c)

        def block(m, carry):
            base = (mine * row_blocks + m) * slots
            left = jnp.concatenate([chosen[column_ref[base + k]] for k in range(slots)], axis=1)
            right = jnp.concatenate([stored[p, m, k] for k in range(slots)], axis=1)
            product = lax.dot_general(left, right, (((1,), (1,)), ((), ())), preferred_element_type=jnp.float32)
            at = x * mu_dev + m * tile + lax.broadcasted_iota(jnp.int32, product.shape, 1)
            product = jnp.where(at < n_basis, product * factor, 0.0)
            slabs[s, :, pl.ds(pl.multiple_of(m * tile, tile), tile)] = product.astype(slabs.dtype)
            return carry

        lax.fori_loop(0, row_blocks, block, 0, unroll=4)

        @pl.when(z < nz - 1)
        def _():
            line_copy(s, 0).start()

        @pl.when(z > 0)
        def _():
            line_copy(s, 1).start()

        spread(s)
        return carry

    lax.fori_loop(0, np_dev, transform, 0)

    events = (nz - 1) * HALVES * 2

    def event(k):
        side, h, far = k % 2, (k // 2) % HALVES, k // (2 * HALVES) + 1
        return z + (2 * side - 1) * far, h, side

    def relay(k):
        origin, h, side = event(k)

        @pl.when((k < events) & (origin >= 0) & (origin < nz))
        def _():
            for q in range(per_half):
                s = slot_of(origin, h * per_half + q, c)
                line_copy(s, 0).wait_recv()

                @pl.when((side == 0) & (z < nz - 1))
                def _():
                    line_copy(s, 0).start()

                @pl.when((side == 1) & (z > 0))
                def _():
                    line_copy(s, 1).start()

                spread(s)

    rows = per_half * 2 * 2 * batch_dev
    width = min(COL_TILE, mu_dev)

    def accumulate(k):
        far_origin, far_h, _ = event(jnp.maximum(k - HALVES, 0))
        origin = jnp.where(k < HALVES, z, far_origin)
        h = jnp.where(k < HALVES, k, far_h)

        @pl.when((origin >= 0) & (origin < nz))
        def _():
            first = slot_of(origin, h * per_half, 0)
            for q in range(per_half):
                pair_copy(slot_of(origin, h * per_half + q, mate)).wait_recv()

            @pl.when(x != my_root)
            def _():
                for q in range(2 * per_half):
                    orb_copy(first + q, 0, 1).wait_recv()
                owner_t[...] = owner[pl.ds(first, 2 * per_half)].reshape(rows, block_rows).T

            @pl.when(x == my_root)
            def _():
                own = slabs[pl.ds(first, 2 * per_half), :, pl.ds(my_offset, block_rows)]
                owner_t[...] = own.reshape(rows, block_rows).T

            def columns(n, carry):
                at = pl.ds(pl.multiple_of(n * width, width), width)
                part = slabs[pl.ds(first, 2 * per_half), :, at].reshape(rows, width)
                out_ref[:, at] += jnp.dot(owner_t[...], part, preferred_element_type=jnp.float32)
                return carry

            lax.fori_loop(0, mu_dev // width, columns, 0)

    def advance(k, carry):
        relay(k)
        accumulate(k)
        return carry

    lax.fori_loop(0, events + HALVES, advance, 0)

    def drain(i, carry):
        origin = i // np_dev
        s = slot_of(origin, i % np_dev, c)
        pair_copy(s).wait_send()

        @pl.when((origin <= z) & (z < nz - 1))
        def _():
            line_copy(s, 0).wait_send()

        @pl.when((origin >= z) & (z > 0))
        def _():
            line_copy(s, 1).wait_send()

        for core in range(2):
            @pl.when(x == root_of(core)[0])
            def _():
                for step in range(1, nx):
                    orb_copy(s, core, step).wait_send()
        return carry

    lax.fori_loop(0, nz * np_dev, drain, 0)


def per_device(nz, nx, b_tiles, nu_block, tile_mask, assignment, metric_factor, orbitals, occupied_index):
    naux_dev, row_blocks, slots, tile, _ = b_tiles.shape
    n_basis = orbitals.shape[1]
    nblocks = (n_basis + tile - 1) // tile
    mu_dev = row_blocks * tile
    batch_dev = occupied_index.shape[0]
    block_rows = nblocks * tile // (nz * 2)
    picked = orbitals.at[occupied_index].get(mode="promise_in_bounds")
    picked = jnp.pad(picked, ((0, 0), (0, nblocks * tile - n_basis)))
    picked = picked.reshape(batch_dev, nblocks, tile).transpose(1, 0, 2)
    column = jnp.where(tile_mask != 0, nu_block, nblocks).reshape(-1)
    np_dev = naux_dev // 2
    nslots = nz * np_dev * 2
    batch = 2 * batch_dev
    rows = np_dev // HALVES * 2 * batch
    vmem = pl.BlockSpec(memory_space=pltpu.VMEM)
    smem = pl.BlockSpec(memory_space=pltpu.SMEM)
    return pl.pallas_call(
        functools.partial(kernel, (nz, nx, n_basis)),
        out_shape=jax.ShapeDtypeStruct((block_rows, mu_dev), jnp.float32),
        in_specs=[vmem, smem, smem, smem, pl.BlockSpec(memory_space=pl.ANY)],
        out_specs=vmem,
        scratch_shapes=[
            pltpu.VMEM((nblocks + 1, batch, tile), jnp.bfloat16),
            pltpu.VMEM((np_dev, row_blocks, slots, tile, tile), jnp.bfloat16),
            pltpu.VMEM((nslots, batch, mu_dev), jnp.bfloat16),
            pltpu.VMEM((nslots, batch, block_rows), jnp.bfloat16),
            pltpu.VMEM((block_rows, rows), jnp.bfloat16),
            pltpu.SemaphoreType.DMA((np_dev,)),
            pltpu.SemaphoreType.DMA((2,)),
            pltpu.SemaphoreType.DMA((2, nslots)),
            pltpu.SemaphoreType.DMA((nslots,)),
            pltpu.SemaphoreType.DMA((nslots,)),
            pltpu.SemaphoreType.DMA((nslots,)),
            pltpu.SemaphoreType.DMA((2, nx - 1, nslots)),
            pltpu.SemaphoreType.DMA((nslots,)),
        ],
        compiler_params=pltpu.CompilerParams(collective_id=0, has_side_effects=True),
    )(picked, column, assignment, metric_factor, b_tiles)


def solution(mesh):
    in_specs = (
        P(("grp", "aux"), "orb", None, None, None),
        P(("grp", "aux"), "orb", None),
        P(("grp", "aux"), "orb", None),
        P(("grp", "aux")),
        P("grp"),
        P("grp", None),
        P(("grp", "occ")),
    )
    out_specs = P(("grp", "aux", "occ"), "orb")
    body = functools.partial(per_device, mesh.shape["aux"], mesh.shape["orb"])
    return jax.shard_map(body, mesh=mesh, in_specs=in_specs, out_specs=out_specs, check_vma=False)
```

```python
import functools
import jax
import jax.numpy as jnp
from jax import lax
from jax.experimental import pallas as pl
from jax.experimental.pallas import tpu as pltpu
from jax.sharding import PartitionSpec as P

MESH = pl.DeviceIdType.MESH
HALVES = 2
COL_TILE = 512
VMEM_GRANT = 44 << 20


def kernel(sizes, picked_ref, column_ref, mask_ref, assign_ref, metric_ref, b_ref, out_ref,
           chosen, stored, slabs, owner, owner_t,
           load_sem, pick_sem, line_send, line_recv, pair_send, pair_recv, orb_send, orb_recv):
    nz, nx, n_basis = sizes
    naux, row_blocks, slots, tile, _ = b_ref.shape
    nblocks, batch_dev, _ = picked_ref.shape
    block_rows, mu_dev = out_ref.shape
    np_dev = naux // 2
    per_half = np_dev // HALVES
    z, x, c = lax.axis_index("aux"), lax.axis_index("orb"), lax.axis_index("occ")
    mate = 1 - c

    def slot_of(origin, p, core):
        return (origin * np_dev + p) * 2 + core

    def root_of(core):
        first = (z * 2 + core) * block_rows
        root = first // mu_dev
        return root, pl.multiple_of(first - root * mu_dev, 128)

    my_root, my_offset = root_of(c)

    def load(p):
        return pltpu.make_async_copy(b_ref.at[c * np_dev + p], stored.at[p], load_sem.at[p])

    for p in range(np_dev):
        load(p).start()

    barrier = pltpu.get_barrier_semaphore()

    def greet(target):
        pl.semaphore_signal(barrier, inc=1, device_id=target, device_id_type=MESH)

    greet({"occ": mate})
    for step in range(1, nx):
        for core in range(2):
            greet({"orb": lax.rem(x + step, nx), "occ": core})

    @pl.when(z > 0)
    def _():
        greet({"aux": z - 1})

    @pl.when(z < nz - 1)
    def _():
        greet({"aux": z + 1})

    chosen[pl.ds(0, nblocks), pl.ds(pl.multiple_of(c * batch_dev, batch_dev), batch_dev), :] = picked_ref[...]
    chosen[nblocks] = jnp.zeros(chosen.shape[1:], chosen.dtype)
    ends = jnp.where(z > 0, 1, 0) + jnp.where(z < nz - 1, 1, 0)
    pl.semaphore_wait(barrier, 1 + 2 * (nx - 1) + ends)

    pick = pltpu.make_async_remote_copy(
        src_ref=picked_ref,
        dst_ref=chosen.at[pl.ds(0, nblocks), pl.ds(pl.multiple_of(c * batch_dev, batch_dev), batch_dev), :],
        send_sem=pick_sem.at[0], recv_sem=pick_sem.at[1],
        device_id={"occ": mate}, device_id_type=MESH)
    pick.start()
    out_ref[...] = jnp.zeros_like(out_ref)

    def line_copy(s, way):
        return pltpu.make_async_remote_copy(
            src_ref=slabs.at[s], dst_ref=slabs.at[s],
            send_sem=line_send.at[way, s], recv_sem=line_recv.at[s],
            device_id={"aux": z + (1 if way == 0 else -1)}, device_id_type=MESH)

    def pair_copy(s):
        return pltpu.make_async_remote_copy(
            src_ref=slabs.at[s], dst_ref=slabs.at[s],
            send_sem=pair_send.at[s], recv_sem=pair_recv.at[s],
            device_id={"occ": mate}, device_id_type=MESH)

    def orb_copy(s, core, step):
        _, offset = root_of(core)
        return pltpu.make_async_remote_copy(
            src_ref=slabs.at[s, :, pl.ds(offset, block_rows)], dst_ref=owner.at[s],
            send_sem=orb_send.at[core, step - 1, s], recv_sem=orb_recv.at[s],
            device_id={"orb": lax.rem(x + step, nx), "occ": core}, device_id_type=MESH)

    def spread(s):
        pair_copy(s).start()
        for core in range(2):
            @pl.when(x == root_of(core)[0])
            def _():
                for step in range(1, nx):
                    orb_copy(s, core, step).start()

    pick.wait()

    def transform(p, carry):
        load(p).wait()
        mine = c * np_dev + p
        factor = metric_ref[assign_ref[mine]]
        s = slot_of(z, p, c)

        def block(m, carry):
            def pick_block(k):
                kept = mask_ref[mine, k, m]
                return chosen[kept * column_ref[mine, k, m] + (1 - kept) * nblocks]

            left = jnp.concatenate([pick_block(k) for k in range(slots)], axis=1)
            right = jnp.concatenate([stored[p, m, k] for k in range(slots)], axis=1)
            product = lax.dot_general(left, right, (((1,), (1,)), ((), ())), preferred_element_type=jnp.float32)
            at = x * mu_dev + m * tile + lax.broadcasted_iota(jnp.int32, product.shape, 1)
            product = jnp.where(at < n_basis, product * factor, 0.0)
            slabs[s, :, pl.ds(pl.multiple_of(m * tile, tile), tile)] = product.astype(slabs.dtype)
            return carry

        lax.fori_loop(0, row_blocks, block, 0, unroll=4)

        @pl.when(z < nz - 1)
        def _():
            line_copy(s, 0).start()

        @pl.when(z > 0)
        def _():
            line_copy(s, 1).start()

        spread(s)
        return carry

    lax.fori_loop(0, np_dev, transform, 0)

    events = (nz - 1) * HALVES * 2

    def event(k):
        side, h, far = k % 2, (k // 2) % HALVES, k // (2 * HALVES) + 1
        return z + (2 * side - 1) * far, h, side

    def relay(k):
        origin, h, side = event(k)

        @pl.when((k < events) & (origin >= 0) & (origin < nz))
        def _():
            for q in range(per_half):
                s = slot_of(origin, h * per_half + q, c)
                line_copy(s, 0).wait_recv()

                @pl.when((side == 0) & (z < nz - 1))
                def _():
                    line_copy(s, 0).start()

                @pl.when((side == 1) & (z > 0))
                def _():
                    line_copy(s, 1).start()

                spread(s)

    rows = per_half * 2 * 2 * batch_dev
    width = min(COL_TILE, mu_dev)

    def accumulate(k):
        far_origin, far_h, _ = event(jnp.maximum(k - HALVES, 0))
        origin = jnp.where(k < HALVES, z, far_origin)
        h = jnp.where(k < HALVES, k, far_h)

        @pl.when((origin >= 0) & (origin < nz))
        def _():
            first = slot_of(origin, h * per_half, 0)
            for q in range(per_half):
                pair_copy(slot_of(origin, h * per_half + q, mate)).wait_recv()

            @pl.when(x != my_root)
            def _():
                for q in range(2 * per_half):
                    orb_copy(first + q, 0, 1).wait_recv()
                owner_t[...] = owner[pl.ds(first, 2 * per_half)].reshape(rows, block_rows).T

            @pl.when(x == my_root)
            def _():
                own = slabs[pl.ds(first, 2 * per_half), :, pl.ds(my_offset, block_rows)]
                owner_t[...] = own.reshape(rows, block_rows).T

            def columns(n, carry):
                at = pl.ds(pl.multiple_of(n * width, width), width)
                part = slabs[pl.ds(first, 2 * per_half), :, at].reshape(rows, width)
                out_ref[:, at] += jnp.dot(owner_t[...], part, preferred_element_type=jnp.float32)
                return carry

            lax.fori_loop(0, mu_dev // width, columns, 0)

    def advance(k, carry):
        relay(k)
        accumulate(k)
        return carry

    lax.fori_loop(0, events + HALVES, advance, 0)

    def drain(i, carry):
        origin = i // np_dev
        s = slot_of(origin, i % np_dev, c)
        pair_copy(s).wait_send()

        @pl.when((origin <= z) & (z < nz - 1))
        def _():
            line_copy(s, 0).wait_send()

        @pl.when((origin >= z) & (z > 0))
        def _():
            line_copy(s, 1).wait_send()

        for core in range(2):
            @pl.when(x == root_of(core)[0])
            def _():
                for step in range(1, nx):
                    orb_copy(s, core, step).wait_send()
        return carry

    lax.fori_loop(0, nz * np_dev, drain, 0)


def per_device(nz, nx, b_tiles, nu_block, tile_mask, assignment, metric_factor, orbitals, occupied_index):
    naux_dev, row_blocks, slots, tile, _ = b_tiles.shape
    n_basis = orbitals.shape[1]
    nblocks = (n_basis + tile - 1) // tile
    mu_dev = row_blocks * tile
    batch_dev = occupied_index.shape[0]
    block_rows = nblocks * tile // (nz * 2)
    picked = orbitals.at[occupied_index].get(mode="promise_in_bounds", wrap_negative_indices=False)
    picked = jnp.pad(picked, ((0, 0), (0, nblocks * tile - n_basis)))
    picked = picked.reshape(batch_dev, nblocks, tile).transpose(1, 0, 2)
    np_dev = naux_dev // 2
    nslots = nz * np_dev * 2
    batch = 2 * batch_dev
    rows = np_dev // HALVES * 2 * batch
    vmem = pl.BlockSpec(memory_space=pltpu.VMEM)
    smem = pl.BlockSpec(memory_space=pltpu.SMEM)
    return pl.pallas_call(
        functools.partial(kernel, (nz, nx, n_basis)),
        out_shape=jax.ShapeDtypeStruct((block_rows, mu_dev), jnp.float32),
        in_specs=[vmem, smem, smem, smem, smem, pl.BlockSpec(memory_space=pltpu.HBM)],
        out_specs=vmem,
        scratch_shapes=[
            pltpu.VMEM((nblocks + 1, batch, tile), jnp.bfloat16),
            pltpu.VMEM((np_dev, row_blocks, slots, tile, tile), jnp.bfloat16),
            pltpu.VMEM((nslots, batch, mu_dev), jnp.bfloat16),
            pltpu.VMEM((nslots, batch, block_rows), jnp.bfloat16),
            pltpu.VMEM((block_rows, rows), jnp.bfloat16),
            pltpu.SemaphoreType.DMA((np_dev,)),
            pltpu.SemaphoreType.DMA((2,)),
            pltpu.SemaphoreType.DMA((2, nslots)),
            pltpu.SemaphoreType.DMA((nslots,)),
            pltpu.SemaphoreType.DMA((nslots,)),
            pltpu.SemaphoreType.DMA((nslots,)),
            pltpu.SemaphoreType.DMA((2, nx - 1, nslots)),
            pltpu.SemaphoreType.DMA((nslots,)),
        ],
        compiler_params=pltpu.CompilerParams(
            collective_id=0, has_side_effects=True,
            vmem_limit_bytes=VMEM_GRANT),
    )(picked, nu_block.transpose(0, 2, 1), tile_mask.transpose(0, 2, 1), assignment, metric_factor, b_tiles)


def solution(mesh):
    in_specs = (
        P(("grp", "aux"), "orb", None, None, None),
        P(("grp", "aux"), "orb", None),
        P(("grp", "aux"), "orb", None),
        P(("grp", "aux")),
        P("grp"),
        P("grp", None),
        P(("grp", "occ")),
    )
    out_specs = P(("grp", "aux", "occ"), "orb")
    body = functools.partial(per_device, mesh.shape["aux"], mesh.shape["orb"])
    return jax.shard_map(body, mesh=mesh, in_specs=in_specs, out_specs=out_specs, check_vma=False)
```

```python
import functools
import jax
import jax.numpy as jnp
from jax import lax
from jax.experimental import pallas as pl
from jax.experimental.pallas import tpu as pltpu
from jax.sharding import PartitionSpec as P

MESH = pl.DeviceIdType.MESH
HALVES = 2
COL_TILE = 512
VMEM_GRANT = 44 << 20


def kernel(sizes, picked_ref, column_ref, mask_ref, assign_ref, metric_ref, b_ref, out_ref,
           chosen, stored, slabs, owner, owner_t,
           load_sem, pick_sem, line_send, line_recv, pair_send, pair_recv, orb_send, orb_recv):
    nz, nx, n_basis = sizes
    naux, row_blocks, slots, tile, _ = b_ref.shape
    nblocks, batch_dev, _ = picked_ref.shape
    block_rows, mu_dev = out_ref.shape
    np_dev = naux // 2
    per_half = np_dev // HALVES
    z, x, c = lax.axis_index("aux"), lax.axis_index("orb"), lax.axis_index("occ")
    mate = 1 - c

    def slot_of(origin, p, core):
        return (origin * np_dev + p) * 2 + core

    def root_of(core):
        first = (z * 2 + core) * block_rows
        root = first // mu_dev
        return root, pl.multiple_of(first - root * mu_dev, 128)

    my_root, my_offset = root_of(c)

    def load(p):
        return pltpu.make_async_copy(b_ref.at[c * np_dev + p], stored.at[p], load_sem.at[p])

    for p in range(np_dev):
        load(p).start()

    barrier = pltpu.get_barrier_semaphore()

    def greet(target):
        pl.semaphore_signal(barrier, inc=1, device_id=target, device_id_type=MESH)

    greet({"occ": mate})
    for step in range(1, nx):
        for core in range(2):
            greet({"orb": lax.rem(x + step, nx), "occ": core})

    @pl.when(z > 0)
    def _():
        greet({"aux": z - 1})

    @pl.when(z < nz - 1)
    def _():
        greet({"aux": z + 1})

    chosen[pl.ds(0, nblocks), pl.ds(pl.multiple_of(c * batch_dev, batch_dev), batch_dev), :] = picked_ref[...]
    chosen[nblocks] = jnp.zeros(chosen.shape[1:], chosen.dtype)
    ends = jnp.where(z > 0, 1, 0) + jnp.where(z < nz - 1, 1, 0)
    pl.semaphore_wait(barrier, 1 + 2 * (nx - 1) + ends)

    pick = pltpu.make_async_remote_copy(
        src_ref=picked_ref,
        dst_ref=chosen.at[pl.ds(0, nblocks), pl.ds(pl.multiple_of(c * batch_dev, batch_dev), batch_dev), :],
        send_sem=pick_sem.at[0], recv_sem=pick_sem.at[1],
        device_id={"occ": mate}, device_id_type=MESH)
    pick.start()
    out_ref[...] = jnp.zeros_like(out_ref)

    def line_copy(s, way):
        return pltpu.make_async_remote_copy(
            src_ref=slabs.at[s], dst_ref=slabs.at[s],
            send_sem=line_send.at[way, s], recv_sem=line_recv.at[s],
            device_id={"aux": z + (1 if way == 0 else -1)}, device_id_type=MESH)

    def pair_copy(s):
        return pltpu.make_async_remote_copy(
            src_ref=slabs.at[s], dst_ref=slabs.at[s],
            send_sem=pair_send.at[s], recv_sem=pair_recv.at[s],
            device_id={"occ": mate}, device_id_type=MESH)

    def orb_copy(s, core, step):
        _, offset = root_of(core)
        return pltpu.make_async_remote_copy(
            src_ref=slabs.at[s, :, pl.ds(offset, block_rows)], dst_ref=owner.at[s],
            send_sem=orb_send.at[core, step - 1, s], recv_sem=orb_recv.at[s],
            device_id={"orb": lax.rem(x + step, nx), "occ": core}, device_id_type=MESH)

    def spread(s):
        pair_copy(s).start()
        for core in range(2):
            @pl.when(x == root_of(core)[0])
            def _():
                for step in range(1, nx):
                    orb_copy(s, core, step).start()

    pick.wait()

    def transform(p, carry):
        load(p).wait()
        mine = c * np_dev + p
        factor = metric_ref[assign_ref[mine]]
        s = slot_of(z, p, c)

        def block(m, carry):
            def pick_block(k):
                kept = mask_ref[mine, k, m]
                return chosen[kept * column_ref[mine, k, m] + (1 - kept) * nblocks]

            left = jnp.concatenate([pick_block(k) for k in range(slots)], axis=1)
            right = jnp.concatenate([stored[p, m, k] for k in range(slots)], axis=1)
            product = lax.dot_general(left, right, (((1,), (1,)), ((), ())), preferred_element_type=jnp.float32)
            at = x * mu_dev + m * tile + lax.broadcasted_iota(jnp.int32, product.shape, 1)
            product = jnp.where(at < n_basis, product * factor, 0.0)
            slabs[s, :, pl.ds(pl.multiple_of(m * tile, tile), tile)] = product.astype(slabs.dtype)
            return carry

        lax.fori_loop(0, row_blocks, block, 0, unroll=4)

        @pl.when(z < nz - 1)
        def _():
            line_copy(s, 0).start()

        @pl.when(z > 0)
        def _():
            line_copy(s, 1).start()

        spread(s)
        return carry

    lax.fori_loop(0, np_dev, transform, 0)

    events = (nz - 1) * HALVES * 2

    def event(k):
        side, h, far = k % 2, (k // 2) % HALVES, k // (2 * HALVES) + 1
        return z + (2 * side - 1) * far, h, side

    def relay(k):
        origin, h, side = event(k)

        @pl.when((k < events) & (origin >= 0) & (origin < nz))
        def _():
            for q in range(per_half):
                s = slot_of(origin, h * per_half + q, c)
                line_copy(s, 0).wait_recv()

                @pl.when((side == 0) & (z < nz - 1))
                def _():
                    line_copy(s, 0).start()

                @pl.when((side == 1) & (z > 0))
                def _():
                    line_copy(s, 1).start()

                spread(s)

    rows = per_half * 2 * 2 * batch_dev
    width = min(COL_TILE, mu_dev)

    def accumulate(k):
        far_origin, far_h, _ = event(jnp.maximum(k - HALVES, 0))
        origin = jnp.where(k < HALVES, z, far_origin)
        h = jnp.where(k < HALVES, k, far_h)

        @pl.when((origin >= 0) & (origin < nz))
        def _():
            first = slot_of(origin, h * per_half, 0)
            for q in range(per_half):
                pair_copy(slot_of(origin, h * per_half + q, mate)).wait_recv()

            @pl.when(x != my_root)
            def _():
                for q in range(2 * per_half):
                    orb_copy(first + q, 0, 1).wait_recv()
                owner_t[...] = owner[pl.ds(first, 2 * per_half)].reshape(rows, block_rows).T

            @pl.when(x == my_root)
            def _():
                own = slabs[pl.ds(first, 2 * per_half), :, pl.ds(my_offset, block_rows)]
                owner_t[...] = own.reshape(rows, block_rows).T

            def columns(n, carry):
                at = pl.ds(pl.multiple_of(n * width, width), width)
                part = slabs[pl.ds(first, 2 * per_half), :, at].reshape(rows, width)
                out_ref[:, at] += jnp.dot(owner_t[...], part, preferred_element_type=jnp.float32)
                return carry

            lax.fori_loop(0, mu_dev // width, columns, 0)

    def advance(k, carry):
        relay(k)
        accumulate(k)
        return carry

    lax.fori_loop(0, events + HALVES, advance, 0)

    def drain(i, carry):
        origin = i // np_dev
        s = slot_of(origin, i % np_dev, c)
        pair_copy(s).wait_send()

        @pl.when((origin <= z) & (z < nz - 1))
        def _():
            line_copy(s, 0).wait_send()

        @pl.when((origin >= z) & (z > 0))
        def _():
            line_copy(s, 1).wait_send()

        for core in range(2):
            @pl.when(x == root_of(core)[0])
            def _():
                for step in range(1, nx):
                    orb_copy(s, core, step).wait_send()
        return carry

    lax.fori_loop(0, nz * np_dev, drain, 0)


def per_device(nz, nx, b_tiles, nu_block, tile_mask, assignment, metric_factor, orbitals, occupied_index):
    naux_dev, row_blocks, slots, tile, _ = b_tiles.shape
    n_basis = orbitals.shape[1]
    nblocks = (n_basis + tile - 1) // tile
    mu_dev = row_blocks * tile
    batch_dev = occupied_index.shape[0]
    block_rows = nblocks * tile // (nz * 2)
    picked = orbitals.at[occupied_index].get(mode="promise_in_bounds", wrap_negative_indices=False)
    picked = jnp.pad(picked, ((0, 0), (0, nblocks * tile - n_basis)))
    picked = picked.reshape(batch_dev, nblocks, tile).transpose(1, 0, 2)
    np_dev = naux_dev // 2
    nslots = nz * np_dev * 2
    batch = 2 * batch_dev
    rows = np_dev // HALVES * 2 * batch
    tables = [nu_block.transpose(0, 2, 1), tile_mask.transpose(0, 2, 1), assignment, metric_factor]
    tables = [pltpu.with_memory_space_constraint(table, pltpu.HBM) for table in tables]
    vmem = pl.BlockSpec(memory_space=pltpu.VMEM)
    smem = pl.BlockSpec(memory_space=pltpu.SMEM)
    return pl.pallas_call(
        functools.partial(kernel, (nz, nx, n_basis)),
        out_shape=jax.ShapeDtypeStruct((block_rows, mu_dev), jnp.float32),
        in_specs=[vmem, smem, smem, smem, smem, pl.BlockSpec(memory_space=pltpu.HBM)],
        out_specs=vmem,
        scratch_shapes=[
            pltpu.VMEM((nblocks + 1, batch, tile), jnp.bfloat16),
            pltpu.VMEM((np_dev, row_blocks, slots, tile, tile), jnp.bfloat16),
            pltpu.VMEM((nslots, batch, mu_dev), jnp.bfloat16),
            pltpu.VMEM((nslots, batch, block_rows), jnp.bfloat16),
            pltpu.VMEM((block_rows, rows), jnp.bfloat16),
            pltpu.SemaphoreType.DMA((np_dev,)),
            pltpu.SemaphoreType.DMA((2,)),
            pltpu.SemaphoreType.DMA((2, nslots)),
            pltpu.SemaphoreType.DMA((nslots,)),
            pltpu.SemaphoreType.DMA((nslots,)),
            pltpu.SemaphoreType.DMA((nslots,)),
            pltpu.SemaphoreType.DMA((2, nx - 1, nslots)),
            pltpu.SemaphoreType.DMA((nslots,)),
        ],
        compiler_params=pltpu.CompilerParams(
            collective_id=0, has_side_effects=True,
            vmem_limit_bytes=VMEM_GRANT),
    )(picked, *tables, b_tiles)


def solution(mesh):
    in_specs = (
        P(("grp", "aux"), "orb", None, None, None),
        P(("grp", "aux"), "orb", None),
        P(("grp", "aux"), "orb", None),
        P(("grp", "aux")),
        P("grp"),
        P("grp", None),
        P(("grp", "occ")),
    )
    out_specs = P(("grp", "aux", "occ"), "orb")
    body = functools.partial(per_device, mesh.shape["aux"], mesh.shape["orb"])
    return jax.shard_map(body, mesh=mesh, in_specs=in_specs, out_specs=out_specs, check_vma=False)
```

```python
import functools
import jax
import jax.numpy as jnp
from jax import lax
from jax.experimental import pallas as pl
from jax.experimental.pallas import tpu as pltpu
from jax.sharding import PartitionSpec as P

MESH = pl.DeviceIdType.MESH
HALVES = 2
COL_TILE = 512
PIECES = 2
VMEM_GRANT = 44 << 20


def kernel(sizes, picked_ref, column_hbm, mask_hbm, assign_hbm, metric_hbm, b_ref, out_ref,
           column_ref, mask_ref, assign_ref, metric_ref, total, chosen, stored, slabs, owner, owner_t,
           table_sem, out_sem, load_sem, pick_sem, line_send, line_recv, pair_send, pair_recv, orb_send, orb_recv):
    nz, nx, n_basis = sizes
    naux, row_blocks, slots, tile, _ = b_ref.shape
    nblocks, batch_dev, _ = picked_ref.shape
    block_rows, mu_dev = out_ref.shape
    np_dev = naux // 2
    piece = 2 * batch_dev // PIECES
    per_half = np_dev // HALVES
    z, x, c = lax.axis_index("aux"), lax.axis_index("orb"), lax.axis_index("occ")
    mate = 1 - c

    def slot_of(origin, p, core):
        return ((origin * np_dev + p) * 2 + core) * PIECES

    def root_of(core):
        first = (z * 2 + core) * block_rows
        root = first // mu_dev
        return root, pl.multiple_of(first - root * mu_dev, 128)

    my_root, my_offset = root_of(c)

    def load(p):
        return pltpu.make_async_copy(b_ref.at[c * np_dev + p], stored.at[p], load_sem.at[p])

    load(0).start()
    tables = [
        pltpu.make_async_copy(source, target, table_sem.at[n])
        for n, (source, target) in enumerate((
            (column_hbm, column_ref), (mask_hbm, mask_ref), (assign_hbm, assign_ref), (metric_hbm, metric_ref)))
    ]
    for table in tables:
        table.start()
    for p in range(1, np_dev):
        load(p).start()

    barrier = pltpu.get_barrier_semaphore()

    def greet(target):
        pl.semaphore_signal(barrier, inc=1, device_id=target, device_id_type=MESH)

    greet({"occ": mate})
    for step in range(1, nx):
        for core in range(2):
            greet({"orb": lax.rem(x + step, nx), "occ": core})

    @pl.when(z > 0)
    def _():
        greet({"aux": z - 1})

    @pl.when(z < nz - 1)
    def _():
        greet({"aux": z + 1})

    chosen[pl.ds(0, nblocks), pl.ds(pl.multiple_of(c * batch_dev, batch_dev), batch_dev), :] = picked_ref[...]
    chosen[nblocks] = jnp.zeros(chosen.shape[1:], chosen.dtype)
    ends = jnp.where(z > 0, 1, 0) + jnp.where(z < nz - 1, 1, 0)
    pl.semaphore_wait(barrier, 1 + 2 * (nx - 1) + ends)

    pick = pltpu.make_async_remote_copy(
        src_ref=picked_ref,
        dst_ref=chosen.at[pl.ds(0, nblocks), pl.ds(pl.multiple_of(c * batch_dev, batch_dev), batch_dev), :],
        send_sem=pick_sem.at[0], recv_sem=pick_sem.at[1],
        device_id={"occ": mate}, device_id_type=MESH)
    pick.start()
    for table in tables:
        table.wait()

    def line_copy(s, way):
        return pltpu.make_async_remote_copy(
            src_ref=slabs.at[s], dst_ref=slabs.at[s],
            send_sem=line_send.at[way, s], recv_sem=line_recv.at[s],
            device_id={"aux": z + (1 if way == 0 else -1)}, device_id_type=MESH)

    def pair_copy(s):
        return pltpu.make_async_remote_copy(
            src_ref=slabs.at[s], dst_ref=slabs.at[s],
            send_sem=pair_send.at[s], recv_sem=pair_recv.at[s],
            device_id={"occ": mate}, device_id_type=MESH)

    def orb_copy(s, core, step):
        _, offset = root_of(core)
        return pltpu.make_async_remote_copy(
            src_ref=slabs.at[s, :, pl.ds(offset, block_rows)], dst_ref=owner.at[s],
            send_sem=orb_send.at[core, step - 1, s], recv_sem=orb_recv.at[s],
            device_id={"orb": lax.rem(x + step, nx), "occ": core}, device_id_type=MESH)

    def spread(s):
        pair_copy(s).start()
        for core in range(2):
            @pl.when(x == root_of(core)[0])
            def _():
                for step in range(1, nx):
                    orb_copy(s, core, step).start()

    pick.wait()

    def transform(p, carry):
        load(p).wait()
        mine = c * np_dev + p
        factor = metric_ref[assign_ref[mine]]
        s = slot_of(z, p, c)

        def block(m, carry):
            def pick_block(k):
                kept = mask_ref[mine, k, m]
                return chosen[kept * column_ref[mine, k, m] + (1 - kept) * nblocks]

            left = jnp.concatenate([pick_block(k) for k in range(slots)], axis=1)
            right = jnp.concatenate([stored[p, m, k] for k in range(slots)], axis=1)
            product = lax.dot_general(left, right, (((1,), (1,)), ((), ())), preferred_element_type=jnp.float32)
            at = x * mu_dev + m * tile + lax.broadcasted_iota(jnp.int32, product.shape, 1)
            product = jnp.where(at < n_basis, product * factor, 0.0)
            for g in range(PIECES):
                part = product[g * piece:(g + 1) * piece]
                slabs[s + g, :, pl.ds(pl.multiple_of(m * tile, tile), tile)] = part.astype(slabs.dtype)
            return carry

        lax.fori_loop(0, row_blocks, block, 0, unroll=4)

        for g in range(PIECES):
            @pl.when(z < nz - 1)
            def _():
                line_copy(s + g, 0).start()

            @pl.when(z > 0)
            def _():
                line_copy(s + g, 1).start()

            spread(s + g)
        return carry

    lax.fori_loop(0, np_dev, transform, 0)

    total[...] = jnp.zeros_like(total)
    events = (nz - 1) * HALVES * 2

    def event(k):
        side, h, far = k % 2, (k // 2) % HALVES, k // (2 * HALVES) + 1
        return z + (2 * side - 1) * far, h, side

    def relay(k):
        origin, h, side = event(k)

        @pl.when((k < events) & (origin >= 0) & (origin < nz))
        def _():
            for q in range(per_half * PIECES):
                s = slot_of(origin, h * per_half + q // PIECES, c) + q % PIECES
                line_copy(s, 0).wait_recv()

                @pl.when((side == 0) & (z < nz - 1))
                def _():
                    line_copy(s, 0).start()

                @pl.when((side == 1) & (z > 0))
                def _():
                    line_copy(s, 1).start()

                spread(s)

    count = per_half * 2 * PIECES
    rows = count * piece
    width = min(COL_TILE, mu_dev)

    before, after = z, nz - 1 - z
    last_side = jnp.where(after >= before, 1, 0)
    last = HALVES + jnp.maximum(before, after) * HALVES * 2 - 2 + last_side

    def out_copy(n):
        at = pl.ds(pl.multiple_of(n * width, width), width)
        return pltpu.make_async_copy(total.at[:, at], out_ref.at[:, at], out_sem.at[n])

    def accumulate(k):
        far_origin, far_h, _ = event(jnp.maximum(k - HALVES, 0))
        origin = jnp.where(k < HALVES, z, far_origin)
        h = jnp.where(k < HALVES, k, far_h)

        @pl.when((origin >= 0) & (origin < nz))
        def _():
            first = slot_of(origin, h * per_half, 0)
            for q in range(per_half * PIECES):
                pair_copy(slot_of(origin, h * per_half + q // PIECES, mate) + q % PIECES).wait_recv()

            @pl.when(x != my_root)
            def _():
                for q in range(count):
                    orb_copy(first + q, 0, 1).wait_recv()
                owner_t[...] = owner[pl.ds(first, count)].reshape(rows, block_rows).T

            @pl.when(x == my_root)
            def _():
                own = slabs[pl.ds(first, count), :, pl.ds(my_offset, block_rows)]
                owner_t[...] = own.reshape(rows, block_rows).T

            def columns(n, carry):
                at = pl.ds(pl.multiple_of(n * width, width), width)
                part = slabs[pl.ds(first, count), :, at].reshape(rows, width)
                total[:, at] += jnp.dot(owner_t[...], part, preferred_element_type=jnp.float32)

                @pl.when(k == last)
                def _():
                    out_copy(n).start()
                return carry

            lax.fori_loop(0, mu_dev // width, columns, 0)

    def advance(k, carry):
        relay(k)
        accumulate(k)
        return carry

    lax.fori_loop(0, events + HALVES, advance, 0)

    def drain(i, carry):
        origin = i // (np_dev * PIECES)
        left = i % (np_dev * PIECES)
        s = slot_of(origin, left // PIECES, c) + left % PIECES
        pair_copy(s).wait_send()

        @pl.when((origin <= z) & (z < nz - 1))
        def _():
            line_copy(s, 0).wait_send()

        @pl.when((origin >= z) & (z > 0))
        def _():
            line_copy(s, 1).wait_send()

        for core in range(2):
            @pl.when(x == root_of(core)[0])
            def _():
                for step in range(1, nx):
                    orb_copy(s, core, step).wait_send()
        return carry

    lax.fori_loop(0, nz * np_dev * PIECES, drain, 0)
    for n in range(mu_dev // width):
        out_copy(n).wait()


def per_device(nz, nx, b_tiles, nu_block, tile_mask, assignment, metric_factor, orbitals, occupied_index):
    naux_dev, row_blocks, slots, tile, _ = b_tiles.shape
    n_basis = orbitals.shape[1]
    nblocks = (n_basis + tile - 1) // tile
    mu_dev = row_blocks * tile
    batch_dev = occupied_index.shape[0]
    block_rows = nblocks * tile // (nz * 2)
    picked = orbitals.at[occupied_index].get(mode="promise_in_bounds", wrap_negative_indices=False)
    picked = jnp.pad(picked, ((0, 0), (0, nblocks * tile - n_basis)))
    picked = picked.reshape(batch_dev, nblocks, tile).transpose(1, 0, 2)
    np_dev = naux_dev // 2
    nslots = nz * np_dev * 2 * PIECES
    piece = 2 * batch_dev // PIECES
    batch = 2 * batch_dev
    rows = np_dev // HALVES * 2 * batch
    tables = [nu_block.transpose(0, 2, 1), tile_mask.transpose(0, 2, 1), assignment, metric_factor]
    tables = [pltpu.with_memory_space_constraint(table, pltpu.HBM) for table in tables]
    vmem = pl.BlockSpec(memory_space=pltpu.VMEM)
    return pl.pallas_call(
        functools.partial(kernel, (nz, nx, n_basis)),
        out_shape=jax.ShapeDtypeStruct((block_rows, mu_dev), jnp.float32),
        in_specs=[vmem] + [pl.BlockSpec(memory_space=pltpu.HBM)] * 5,
        out_specs=pl.BlockSpec(memory_space=pl.ANY),
        scratch_shapes=[pltpu.SMEM(table.shape, table.dtype) for table in tables] + [
            pltpu.VMEM((block_rows, mu_dev), jnp.float32),
            pltpu.VMEM((nblocks + 1, batch, tile), jnp.bfloat16),
            pltpu.VMEM((np_dev, row_blocks, slots, tile, tile), jnp.bfloat16),
            pltpu.VMEM((nslots, piece, mu_dev), jnp.bfloat16),
            pltpu.VMEM((nslots, piece, block_rows), jnp.bfloat16),
            pltpu.VMEM((block_rows, rows), jnp.bfloat16),
            pltpu.SemaphoreType.DMA((len(tables),)),
            pltpu.SemaphoreType.DMA((mu_dev // min(COL_TILE, mu_dev),)),
            pltpu.SemaphoreType.DMA((np_dev,)),
            pltpu.SemaphoreType.DMA((2,)),
            pltpu.SemaphoreType.DMA((2, nslots)),
            pltpu.SemaphoreType.DMA((nslots,)),
            pltpu.SemaphoreType.DMA((nslots,)),
            pltpu.SemaphoreType.DMA((nslots,)),
            pltpu.SemaphoreType.DMA((2, nx - 1, nslots)),
            pltpu.SemaphoreType.DMA((nslots,)),
        ],
        compiler_params=pltpu.CompilerParams(
            collective_id=0, has_side_effects=True,
            vmem_limit_bytes=VMEM_GRANT),
    )(picked, *tables, b_tiles)


def solution(mesh):
    in_specs = (
        P(("grp", "aux"), "orb", None, None, None),
        P(("grp", "aux"), "orb", None),
        P(("grp", "aux"), "orb", None),
        P(("grp", "aux")),
        P("grp"),
        P("grp", None),
        P(("grp", "occ")),
    )
    out_specs = P(("grp", "aux", "occ"), "orb")
    body = functools.partial(per_device, mesh.shape["aux"], mesh.shape["orb"])
    return jax.shard_map(body, mesh=mesh, in_specs=in_specs, out_specs=out_specs, check_vma=False)
```

```python
import functools
import jax
import jax.numpy as jnp
from jax import lax
from jax.experimental import pallas as pl
from jax.experimental.pallas import tpu as pltpu
from jax.sharding import PartitionSpec as P

MESH = pl.DeviceIdType.MESH
HALVES = 2
COL_TILE = 512
PIECES = 1
VMEM_GRANT = 44 << 20


def kernel(sizes, picked_ref, column_hbm, mask_hbm, assign_hbm, metric_hbm, b_ref, out_ref,
           column_ref, mask_ref, assign_ref, metric_ref, total, chosen, stored, slabs, owner, owner_t,
           table_sem, out_sem, load_sem, pick_sem, line_send, line_recv, pair_send, pair_recv, orb_send, orb_recv):
    nz, nx, n_basis = sizes
    naux, row_blocks, slots, tile, _ = b_ref.shape
    nblocks, batch_dev, _ = picked_ref.shape
    block_rows, mu_dev = out_ref.shape
    np_dev = naux // 2
    piece = 2 * batch_dev // PIECES
    per_half = np_dev // HALVES
    z, x, c = lax.axis_index("aux"), lax.axis_index("orb"), lax.axis_index("occ")
    mate = 1 - c

    def slot_of(origin, p, core):
        return ((origin * np_dev + p) * 2 + core) * PIECES

    def root_of(core):
        first = (z * 2 + core) * block_rows
        root = first // mu_dev
        return root, pl.multiple_of(first - root * mu_dev, 128)

    my_root, my_offset = root_of(c)

    def load(p):
        return pltpu.make_async_copy(b_ref.at[c * np_dev + p], stored.at[p], load_sem.at[p])

    load(0).start()
    tables = [
        pltpu.make_async_copy(source, target, table_sem.at[n])
        for n, (source, target) in enumerate((
            (column_hbm, column_ref), (mask_hbm, mask_ref), (assign_hbm, assign_ref), (metric_hbm, metric_ref)))
    ]
    for table in tables:
        table.start()
    for p in range(1, np_dev):
        load(p).start()

    barrier = pltpu.get_barrier_semaphore()

    def greet(target):
        pl.semaphore_signal(barrier, inc=1, device_id=target, device_id_type=MESH)

    greet({"occ": mate})
    for step in range(1, nx):
        for core in range(2):
            greet({"orb": lax.rem(x + step, nx), "occ": core})

    @pl.when(z > 0)
    def _():
        greet({"aux": z - 1})

    @pl.when(z < nz - 1)
    def _():
        greet({"aux": z + 1})

    chosen[pl.ds(0, nblocks), pl.ds(pl.multiple_of(c * batch_dev, batch_dev), batch_dev), :] = picked_ref[...]
    chosen[nblocks] = jnp.zeros(chosen.shape[1:], chosen.dtype)
    ends = jnp.where(z > 0, 1, 0) + jnp.where(z < nz - 1, 1, 0)
    pl.semaphore_wait(barrier, 1 + 2 * (nx - 1) + ends)

    pick = pltpu.make_async_remote_copy(
        src_ref=picked_ref,
        dst_ref=chosen.at[pl.ds(0, nblocks), pl.ds(pl.multiple_of(c * batch_dev, batch_dev), batch_dev), :],
        send_sem=pick_sem.at[0], recv_sem=pick_sem.at[1],
        device_id={"occ": mate}, device_id_type=MESH)
    pick.start()
    for table in tables:
        table.wait()

    def line_copy(s, way):
        return pltpu.make_async_remote_copy(
            src_ref=slabs.at[s], dst_ref=slabs.at[s],
            send_sem=line_send.at[way, s], recv_sem=line_recv.at[s],
            device_id={"aux": z + (1 if way == 0 else -1)}, device_id_type=MESH)

    def pair_copy(s):
        return pltpu.make_async_remote_copy(
            src_ref=slabs.at[s], dst_ref=slabs.at[s],
            send_sem=pair_send.at[s], recv_sem=pair_recv.at[s],
            device_id={"occ": mate}, device_id_type=MESH)

    def orb_copy(s, core, step):
        _, offset = root_of(core)
        return pltpu.make_async_remote_copy(
            src_ref=slabs.at[s, :, pl.ds(offset, block_rows)], dst_ref=owner.at[s],
            send_sem=orb_send.at[core, step - 1, s], recv_sem=orb_recv.at[s],
            device_id={"orb": lax.rem(x + step, nx), "occ": core}, device_id_type=MESH)

    def spread(s):
        pair_copy(s).start()
        for core in range(2):
            @pl.when(x == root_of(core)[0])
            def _():
                for step in range(1, nx):
                    orb_copy(s, core, step).start()

    pick.wait()

    def transform(p, carry):
        load(p).wait()
        mine = c * np_dev + p
        factor = metric_ref[assign_ref[mine]]
        s = slot_of(z, p, c)

        def block(m, carry):
            def pick_block(k):
                kept = mask_ref[mine, k, m]
                return chosen[kept * column_ref[mine, k, m] + (1 - kept) * nblocks]

            left = jnp.concatenate([pick_block(k) for k in range(slots)], axis=1)
            right = jnp.concatenate([stored[p, m, k] for k in range(slots)], axis=1)
            product = lax.dot_general(left, right, (((1,), (1,)), ((), ())), preferred_element_type=jnp.float32)
            at = x * mu_dev + m * tile + lax.broadcasted_iota(jnp.int32, product.shape, 1)
            product = jnp.where(at < n_basis, product * factor, 0.0)
            for g in range(PIECES):
                part = product[g * piece:(g + 1) * piece]
                slabs[s + g, :, pl.ds(pl.multiple_of(m * tile, tile), tile)] = part.astype(slabs.dtype)
            return carry

        lax.fori_loop(0, row_blocks, block, 0, unroll=4)

        for g in range(PIECES):
            @pl.when(z < nz - 1)
            def _():
                line_copy(s + g, 0).start()

            @pl.when(z > 0)
            def _():
                line_copy(s + g, 1).start()

            spread(s + g)
        return carry

    lax.fori_loop(0, np_dev, transform, 0)

    total[...] = jnp.zeros_like(total)
    events = (nz - 1) * HALVES * 2

    def event(k):
        side, h, far = k % 2, (k // 2) % HALVES, k // (2 * HALVES) + 1
        return z + (2 * side - 1) * far, h, side

    def relay(k):
        origin, h, side = event(k)

        @pl.when((k < events) & (origin >= 0) & (origin < nz))
        def _():
            for q in range(per_half * PIECES):
                s = slot_of(origin, h * per_half + q // PIECES, c) + q % PIECES
                line_copy(s, 0).wait_recv()

                @pl.when((side == 0) & (z < nz - 1))
                def _():
                    line_copy(s, 0).start()

                @pl.when((side == 1) & (z > 0))
                def _():
                    line_copy(s, 1).start()

                spread(s)

    count = per_half * 2 * PIECES
    rows = count * piece
    width = min(COL_TILE, mu_dev)

    before, after = z, nz - 1 - z
    last_side = jnp.where(after >= before, 1, 0)
    last = HALVES + jnp.maximum(before, after) * HALVES * 2 - 2 + last_side

    def out_copy(n):
        at = pl.ds(pl.multiple_of(n * width, width), width)
        return pltpu.make_async_copy(total.at[:, at], out_ref.at[:, at], out_sem.at[n])

    def accumulate(k):
        far_origin, far_h, _ = event(jnp.maximum(k - HALVES, 0))
        origin = jnp.where(k < HALVES, z, far_origin)
        h = jnp.where(k < HALVES, k, far_h)

        @pl.when((origin >= 0) & (origin < nz))
        def _():
            first = slot_of(origin, h * per_half, 0)
            for q in range(per_half * PIECES):
                pair_copy(slot_of(origin, h * per_half + q // PIECES, mate) + q % PIECES).wait_recv()

            @pl.when(x != my_root)
            def _():
                for q in range(count):
                    orb_copy(first + q, 0, 1).wait_recv()
                owner_t[...] = owner[pl.ds(first, count)].reshape(rows, block_rows).T

            @pl.when(x == my_root)
            def _():
                own = slabs[pl.ds(first, count), :, pl.ds(my_offset, block_rows)]
                owner_t[...] = own.reshape(rows, block_rows).T

            def columns(n, carry):
                at = pl.ds(pl.multiple_of(n * width, width), width)
                part = slabs[pl.ds(first, count), :, at].reshape(rows, width)
                total[:, at] += jnp.dot(owner_t[...], part, preferred_element_type=jnp.float32)

                @pl.when(k == last)
                def _():
                    out_copy(n).start()
                return carry

            lax.fori_loop(0, mu_dev // width, columns, 0)

    def advance(k, carry):
        relay(k)
        accumulate(k)
        return carry

    lax.fori_loop(0, events + HALVES, advance, 0)

    def drain(i, carry):
        origin = i // (np_dev * PIECES)
        left = i % (np_dev * PIECES)
        s = slot_of(origin, left // PIECES, c) + left % PIECES
        pair_copy(s).wait_send()

        @pl.when((origin <= z) & (z < nz - 1))
        def _():
            line_copy(s, 0).wait_send()

        @pl.when((origin >= z) & (z > 0))
        def _():
            line_copy(s, 1).wait_send()

        for core in range(2):
            @pl.when(x == root_of(core)[0])
            def _():
                for step in range(1, nx):
                    orb_copy(s, core, step).wait_send()
        return carry

    lax.fori_loop(0, nz * np_dev * PIECES, drain, 0)
    for n in range(mu_dev // width):
        out_copy(n).wait()


def per_device(nz, nx, b_tiles, nu_block, tile_mask, assignment, metric_factor, orbitals, occupied_index):
    naux_dev, row_blocks, slots, tile, _ = b_tiles.shape
    n_basis = orbitals.shape[1]
    nblocks = (n_basis + tile - 1) // tile
    mu_dev = row_blocks * tile
    batch_dev = occupied_index.shape[0]
    block_rows = nblocks * tile // (nz * 2)
    picked = orbitals.at[occupied_index].get(mode="promise_in_bounds", wrap_negative_indices=False)
    picked = jnp.pad(picked, ((0, 0), (0, nblocks * tile - n_basis)))
    picked = picked.reshape(batch_dev, nblocks, tile).transpose(1, 0, 2)
    np_dev = naux_dev // 2
    nslots = nz * np_dev * 2 * PIECES
    piece = 2 * batch_dev // PIECES
    batch = 2 * batch_dev
    rows = np_dev // HALVES * 2 * batch
    tables = [nu_block.transpose(0, 2, 1), tile_mask.transpose(0, 2, 1), assignment, metric_factor]
    tables = [pltpu.with_memory_space_constraint(table, pltpu.HBM) for table in tables]
    vmem = pl.BlockSpec(memory_space=pltpu.VMEM)
    return pl.pallas_call(
        functools.partial(kernel, (nz, nx, n_basis)),
        out_shape=jax.ShapeDtypeStruct((block_rows, mu_dev), jnp.float32),
        in_specs=[vmem] + [pl.BlockSpec(memory_space=pltpu.HBM)] * 5,
        out_specs=pl.BlockSpec(memory_space=pl.ANY),
        scratch_shapes=[pltpu.SMEM(table.shape, table.dtype) for table in tables] + [
            pltpu.VMEM((block_rows, mu_dev), jnp.float32),
            pltpu.VMEM((nblocks + 1, batch, tile), jnp.bfloat16),
            pltpu.VMEM((np_dev, row_blocks, slots, tile, tile), jnp.bfloat16),
            pltpu.VMEM((nslots, piece, mu_dev), jnp.bfloat16),
            pltpu.VMEM((nslots, piece, block_rows), jnp.bfloat16),
            pltpu.VMEM((block_rows, rows), jnp.bfloat16),
            pltpu.SemaphoreType.DMA((len(tables),)),
            pltpu.SemaphoreType.DMA((mu_dev // min(COL_TILE, mu_dev),)),
            pltpu.SemaphoreType.DMA((np_dev,)),
            pltpu.SemaphoreType.DMA((2,)),
            pltpu.SemaphoreType.DMA((2, nslots)),
            pltpu.SemaphoreType.DMA((nslots,)),
            pltpu.SemaphoreType.DMA((nslots,)),
            pltpu.SemaphoreType.DMA((nslots,)),
            pltpu.SemaphoreType.DMA((2, nx - 1, nslots)),
            pltpu.SemaphoreType.DMA((nslots,)),
        ],
        compiler_params=pltpu.CompilerParams(
            collective_id=0, has_side_effects=True,
            vmem_limit_bytes=VMEM_GRANT),
    )(picked, *tables, b_tiles)


def solution(mesh):
    in_specs = (
        P(("grp", "aux"), "orb", None, None, None),
        P(("grp", "aux"), "orb", None),
        P(("grp", "aux"), "orb", None),
        P(("grp", "aux")),
        P("grp"),
        P("grp", None),
        P(("grp", "occ")),
    )
    out_specs = P(("grp", "aux", "occ"), "orb")
    body = functools.partial(per_device, mesh.shape["aux"], mesh.shape["orb"])
    return jax.shard_map(body, mesh=mesh, in_specs=in_specs, out_specs=out_specs, check_vma=False)
```

```python
import functools
import jax
import jax.numpy as jnp
from jax import lax
from jax.experimental import pallas as pl
from jax.experimental.pallas import tpu as pltpu
from jax.sharding import PartitionSpec as P

MESH = pl.DeviceIdType.MESH
HALVES = 2
COL_TILE = 512
PIECES = 1
VMEM_GRANT = 44 << 20


def kernel(sizes, picked_ref, column_hbm, mask_hbm, assign_hbm, metric_hbm, b_ref, out_ref,
           column_ref, mask_ref, assign_ref, metric_ref, total, chosen, stored, slabs, owner, owner_t,
           table_sem, out_sem, load_sem, pick_sem, line_send, line_recv, pair_send, pair_recv, orb_send, orb_recv):
    nz, nx, n_basis = sizes
    naux, row_blocks, slots, tile, _ = b_ref.shape
    nblocks, batch_dev, _ = picked_ref.shape
    block_rows, mu_dev = out_ref.shape
    np_dev = naux // 2
    piece = 2 * batch_dev // PIECES
    per_half = np_dev // HALVES
    z, x, c = lax.axis_index("aux"), lax.axis_index("orb"), lax.axis_index("occ")
    mate = 1 - c

    def slot_of(origin, p, core):
        return ((origin * np_dev + p) * 2 + core) * PIECES

    def root_of(core):
        first = (z * 2 + core) * block_rows
        root = first // mu_dev
        return root, pl.multiple_of(first - root * mu_dev, 128)

    my_root, my_offset = root_of(c)

    def load(p):
        return pltpu.make_async_copy(b_ref.at[c * np_dev + p], stored.at[p], load_sem.at[p])

    load(0).start()
    tables = [
        pltpu.make_async_copy(source, target, table_sem.at[n])
        for n, (source, target) in enumerate((
            (column_hbm, column_ref), (mask_hbm, mask_ref), (assign_hbm, assign_ref), (metric_hbm, metric_ref)))
    ]
    for table in tables:
        table.start()
    for p in range(1, np_dev):
        load(p).start()

    barrier = pltpu.get_barrier_semaphore()

    def greet(target):
        pl.semaphore_signal(barrier, inc=1, device_id=target, device_id_type=MESH)

    greet({"occ": mate})
    for step in range(1, nx):
        for core in range(2):
            greet({"orb": lax.rem(x + step, nx), "occ": core})

    @pl.when(z > 0)
    def _():
        greet({"aux": z - 1})

    @pl.when(z < nz - 1)
    def _():
        greet({"aux": z + 1})

    chosen[pl.ds(0, nblocks), pl.ds(pl.multiple_of(c * batch_dev, batch_dev), batch_dev), :] = picked_ref[...]
    chosen[nblocks] = jnp.zeros(chosen.shape[1:], chosen.dtype)
    ends = jnp.where(z > 0, 1, 0) + jnp.where(z < nz - 1, 1, 0)
    pl.semaphore_wait(barrier, 1 + 2 * (nx - 1) + ends)

    pick = pltpu.make_async_remote_copy(
        src_ref=picked_ref,
        dst_ref=chosen.at[pl.ds(0, nblocks), pl.ds(pl.multiple_of(c * batch_dev, batch_dev), batch_dev), :],
        send_sem=pick_sem.at[0], recv_sem=pick_sem.at[1],
        device_id={"occ": mate}, device_id_type=MESH)
    pick.start()
    for table in tables:
        table.wait()

    def line_copy(s, way):
        return pltpu.make_async_remote_copy(
            src_ref=slabs.at[s], dst_ref=slabs.at[s],
            send_sem=line_send.at[way, s], recv_sem=line_recv.at[s],
            device_id={"aux": z + (1 if way == 0 else -1)}, device_id_type=MESH)

    def pair_copy(s):
        return pltpu.make_async_remote_copy(
            src_ref=slabs.at[s], dst_ref=slabs.at[s],
            send_sem=pair_send.at[s], recv_sem=pair_recv.at[s],
            device_id={"occ": mate}, device_id_type=MESH)

    def orb_copy(s, core, step):
        _, offset = root_of(core)
        return pltpu.make_async_remote_copy(
            src_ref=slabs.at[s, :, pl.ds(offset, block_rows)], dst_ref=owner.at[s],
            send_sem=orb_send.at[core, step - 1, s], recv_sem=orb_recv.at[s],
            device_id={"orb": lax.rem(x + step, nx), "occ": core}, device_id_type=MESH)

    def spread(s):
        pair_copy(s).start()
        for core in range(2):
            @pl.when(x == root_of(core)[0])
            def _():
                for step in range(1, nx):
                    orb_copy(s, core, step).start()

    pick.wait()

    def transform(p, carry):
        load(p).wait()
        mine = c * np_dev + p
        factor = metric_ref[assign_ref[mine]]
        s = slot_of(z, p, c)

        def block(m, carry):
            def pick_block(k):
                kept = mask_ref[mine, k, m]
                return chosen[kept * column_ref[mine, k, m] + (1 - kept) * nblocks]

            left = jnp.concatenate([pick_block(k) for k in range(slots)], axis=1)
            right = jnp.concatenate([stored[p, m, k] for k in range(slots)], axis=1)
            product = lax.dot_general(left, right, (((1,), (1,)), ((), ())), preferred_element_type=jnp.float32)
            at = x * mu_dev + m * tile + lax.broadcasted_iota(jnp.int32, product.shape, 1)
            product = jnp.where(at < n_basis, product * factor, 0.0)
            for g in range(PIECES):
                part = product[g * piece:(g + 1) * piece]
                slabs[s + g, :, pl.ds(pl.multiple_of(m * tile, tile), tile)] = part.astype(slabs.dtype)
            return carry

        lax.fori_loop(0, row_blocks, block, 0, unroll=4)

        for g in range(PIECES):
            @pl.when(z < nz - 1)
            def _():
                line_copy(s + g, 0).start()

            @pl.when(z > 0)
            def _():
                line_copy(s + g, 1).start()

            spread(s + g)
        return carry

    lax.fori_loop(0, np_dev, transform, 0)

    total[...] = jnp.zeros_like(total)
    events = (nz - 1) * HALVES * 2

    def event(k):
        side, h, far = k % 2, (k // 2) % HALVES, k // (2 * HALVES) + 1
        return z + (2 * side - 1) * far, h, side

    def relay(k):
        origin, h, side = event(k)

        @pl.when((k < events) & (origin >= 0) & (origin < nz))
        def _():
            for q in range(per_half * PIECES):
                s = slot_of(origin, h * per_half + q // PIECES, c) + q % PIECES
                line_copy(s, 0).wait_recv()

                @pl.when((side == 0) & (z < nz - 1))
                def _():
                    line_copy(s, 0).start()

                @pl.when((side == 1) & (z > 0))
                def _():
                    line_copy(s, 1).start()

                spread(s)

    count = per_half * 2 * PIECES
    rows = count * piece
    width = min(COL_TILE, mu_dev)

    before, after = z, nz - 1 - z
    last_side = jnp.where(after >= before, 1, 0)
    last = HALVES + jnp.maximum(before, after) * HALVES * 2 - 2 + last_side

    def out_copy(n):
        at = pl.ds(pl.multiple_of(n * width, width), width)
        return pltpu.make_async_copy(total.at[:, at], out_ref.at[:, at], out_sem.at[n])

    def accumulate(k):
        far_origin, far_h, _ = event(jnp.maximum(k - HALVES, 0))
        origin = jnp.where(k < HALVES, z, far_origin)
        h = jnp.where(k < HALVES, k, far_h)

        @pl.when((origin >= 0) & (origin < nz))
        def _():
            first = slot_of(origin, h * per_half, 0)
            for q in range(per_half * PIECES):
                pair_copy(slot_of(origin, h * per_half + q // PIECES, mate) + q % PIECES).wait_recv()

            @pl.when(x != my_root)
            def _():
                for q in range(count):
                    orb_copy(first + q, 0, 1).wait_recv()
                owner_t[...] = owner[pl.ds(first, count)].reshape(rows, block_rows).T

            @pl.when(x == my_root)
            def _():
                own = slabs[pl.ds(first, count), :, pl.ds(my_offset, block_rows)]
                owner_t[...] = own.reshape(rows, block_rows).T

            def columns(n, carry):
                at = pl.ds(pl.multiple_of(n * width, width), width)
                part = slabs[pl.ds(first, count), :, at].reshape(rows, width)
                total[:, at] += jnp.dot(owner_t[...], part, preferred_element_type=jnp.float32)

                @pl.when(k == last)
                def _():
                    out_copy(n).start()
                return carry

            lax.fori_loop(0, mu_dev // width, columns, 0)

    def advance(k, carry):
        relay(k)
        accumulate(k + HALVES - 1)
        return carry

    for h in range(HALVES - 1):
        accumulate(h)
    lax.fori_loop(0, events + 1, advance, 0)

    def drain(i, carry):
        origin = i // (np_dev * PIECES)
        left = i % (np_dev * PIECES)
        s = slot_of(origin, left // PIECES, c) + left % PIECES
        pair_copy(s).wait_send()

        @pl.when((origin <= z) & (z < nz - 1))
        def _():
            line_copy(s, 0).wait_send()

        @pl.when((origin >= z) & (z > 0))
        def _():
            line_copy(s, 1).wait_send()

        for core in range(2):
            @pl.when(x == root_of(core)[0])
            def _():
                for step in range(1, nx):
                    orb_copy(s, core, step).wait_send()
        return carry

    lax.fori_loop(0, nz * np_dev * PIECES, drain, 0)
    for n in range(mu_dev // width):
        out_copy(n).wait()


def per_device(nz, nx, b_tiles, nu_block, tile_mask, assignment, metric_factor, orbitals, occupied_index):
    naux_dev, row_blocks, slots, tile, _ = b_tiles.shape
    n_basis = orbitals.shape[1]
    nblocks = (n_basis + tile - 1) // tile
    mu_dev = row_blocks * tile
    batch_dev = occupied_index.shape[0]
    block_rows = nblocks * tile // (nz * 2)
    picked = orbitals.at[occupied_index].get(mode="promise_in_bounds", wrap_negative_indices=False)
    picked = jnp.pad(picked, ((0, 0), (0, nblocks * tile - n_basis)))
    picked = picked.reshape(batch_dev, nblocks, tile).transpose(1, 0, 2)
    np_dev = naux_dev // 2
    nslots = nz * np_dev * 2 * PIECES
    piece = 2 * batch_dev // PIECES
    batch = 2 * batch_dev
    rows = np_dev // HALVES * 2 * batch
    tables = [nu_block.transpose(0, 2, 1), tile_mask.transpose(0, 2, 1), assignment, metric_factor]
    tables = [pltpu.with_memory_space_constraint(table, pltpu.HBM) for table in tables]
    vmem = pl.BlockSpec(memory_space=pltpu.VMEM)
    return pl.pallas_call(
        functools.partial(kernel, (nz, nx, n_basis)),
        out_shape=jax.ShapeDtypeStruct((block_rows, mu_dev), jnp.float32),
        in_specs=[vmem] + [pl.BlockSpec(memory_space=pltpu.HBM)] * 5,
        out_specs=pl.BlockSpec(memory_space=pl.ANY),
        scratch_shapes=[pltpu.SMEM(table.shape, table.dtype) for table in tables] + [
            pltpu.VMEM((block_rows, mu_dev), jnp.float32),
            pltpu.VMEM((nblocks + 1, batch, tile), jnp.bfloat16),
            pltpu.VMEM((np_dev, row_blocks, slots, tile, tile), jnp.bfloat16),
            pltpu.VMEM((nslots, piece, mu_dev), jnp.bfloat16),
            pltpu.VMEM((nslots, piece, block_rows), jnp.bfloat16),
            pltpu.VMEM((block_rows, rows), jnp.bfloat16),
            pltpu.SemaphoreType.DMA((len(tables),)),
            pltpu.SemaphoreType.DMA((mu_dev // min(COL_TILE, mu_dev),)),
            pltpu.SemaphoreType.DMA((np_dev,)),
            pltpu.SemaphoreType.DMA((2,)),
            pltpu.SemaphoreType.DMA((2, nslots)),
            pltpu.SemaphoreType.DMA((nslots,)),
            pltpu.SemaphoreType.DMA((nslots,)),
            pltpu.SemaphoreType.DMA((nslots,)),
            pltpu.SemaphoreType.DMA((2, nx - 1, nslots)),
            pltpu.SemaphoreType.DMA((nslots,)),
        ],
        compiler_params=pltpu.CompilerParams(
            collective_id=0, has_side_effects=True,
            vmem_limit_bytes=VMEM_GRANT),
    )(picked, *tables, b_tiles)


def solution(mesh):
    in_specs = (
        P(("grp", "aux"), "orb", None, None, None),
        P(("grp", "aux"), "orb", None),
        P(("grp", "aux"), "orb", None),
        P(("grp", "aux")),
        P("grp"),
        P("grp", None),
        P(("grp", "occ")),
    )
    out_specs = P(("grp", "aux", "occ"), "orb")
    body = functools.partial(per_device, mesh.shape["aux"], mesh.shape["orb"])
    return jax.shard_map(body, mesh=mesh, in_specs=in_specs, out_specs=out_specs, check_vma=False)
```
